32 devices in a mesh: fsdp: 4 (over y, x), ctx: 8 (over z, core).
Axes of the slice: x: 2, y: 2, z: 4, core: 2. Of those that a mesh axis runs over, the one named last changes fastest.
Arguments:
- tokens: bfloat16 [4, 1024, 5376], P('fsdp', 'ctx'), may hold values from -6 to 6
- pre_gain: float32 [5376], replicated, may hold values from 0.1 to 1.9
- w_query: bfloat16 [5376, 3072], P(None, 'fsdp'), may hold values from -0.078125 to 0.078125
- key_weight: bfloat16 [5376, 1536], P(None, 'fsdp'), may hold values from -0.078125 to 0.078125
- value_weight: bfloat16 [5376, 1536], P(None, 'fsdp'), may hold values from -0.078125 to 0.078125
- query_norm_gain: float32 [128], replicated, may hold values from 0.1 to 1.9
- key_gain: float32 [128], replicated, may hold values from 0.1 to 1.9
- w_out: bfloat16 [3072, 5376], P('fsdp'), may hold values from -0.109375 to 0.109375
- post_gain: float32 [5376], replicated, may hold values from 0.1 to 1.9
Outputs:
- layer_out: bfloat16 [4, 1024, 5376], P('fsdp', 'ctx')
The draws below stay inside these ranges and needn't reach their ends.
All inputs are finite; a program needn't handle non-finite values.
Results may differ from the reference program's by a relative error of at most 0.012.
Values may be sent and summed in bfloat16 or wider, within the bound.
A program may use at most 128 MiB of HBM per device.

```python
import jax
import jax.numpy as jnp
from jax import lax

MODEL_WIDTH = 5376
QUERY_HEADS = 24
KEY_VALUE_HEADS = 12
HEAD_SIZE = 128
WINDOW = 1024
LEN = 1024
DOCS = 4
N_FSDP = 4


def level_of(key, dims, shards, least, top_value):
    level, own = 1.0, jax.random.fold_in(key, 6)
    for axis_at, shards_of in shards:
        heights = jnp.exp(jax.random.uniform(jax.random.fold_in(own, axis_at), (shards_of,), jnp.float32, least / len(shards), top_value / len(shards)))
        level = level * jnp.repeat(heights, dims[axis_at] // shards_of).reshape([-1 if axis == axis_at else 1 for axis in range(len(dims))])
    return level


def gaussian(stream_key, extent, scale, reach, split=(), held_as=jnp.bfloat16):
    values = jax.random.normal(stream_key, extent, jnp.float32) * scale
    if len(split) > 0:
        values = level_of(stream_key, extent, split, -0.22, 0.18) * values
    return jnp.clip(values, min=-reach, max=reach).astype(held_as)


def setup_inputs(seed: int = 0) -> dict:
    splits = jax.random.split(jax.random.key(seed), 10)
    tokens = gaussian(splits[0], (DOCS, LEN, MODEL_WIDTH), 1.0, 6.0, ((0, 4), (1, 8)))
    pre_gain = jnp.clip(1.0 + 0.18 * jax.random.normal(splits[1], (MODEL_WIDTH,), jnp.float32), 0.1, 1.9)
    w_query = gaussian(splits[2], (MODEL_WIDTH, QUERY_HEADS * HEAD_SIZE), MODEL_WIDTH ** -0.5, 0.078125, ((1, 4),))
    key_weight = gaussian(splits[3], (MODEL_WIDTH, KEY_VALUE_HEADS * HEAD_SIZE), MODEL_WIDTH ** -0.5, 0.078125, ((1, 4),))
    value_weight = gaussian(splits[4], (MODEL_WIDTH, KEY_VALUE_HEADS * HEAD_SIZE), MODEL_WIDTH ** -0.5, 0.078125, ((1, 4),))
    query_norm_gain = jnp.clip(1.0 + 0.18 * jax.random.normal(splits[5], (HEAD_SIZE,), jnp.float32), 0.1, 1.9)
    key_gain = jnp.clip(1.0 + 0.18 * jax.random.normal(splits[6], (HEAD_SIZE,), jnp.float32), 0.1, 1.9)
    w_out = gaussian(splits[7], (QUERY_HEADS * HEAD_SIZE, MODEL_WIDTH), (QUERY_HEADS * HEAD_SIZE) ** -0.5, 0.109375, ((0, 4),))
    post_gain = jnp.clip(1.0 + 0.18 * jax.random.normal(splits[8], (MODEL_WIDTH,), jnp.float32), 0.1, 1.9)
    return dict(tokens=tokens, pre_gain=pre_gain, w_query=w_query, key_weight=key_weight, value_weight=value_weight, query_norm_gain=query_norm_gain, key_gain=key_gain, w_out=w_out, post_gain=post_gain)


epsilon = 1e-06
score_scale = 168.0 ** (-0.5)

def root_mean_norm(values, gain):
    mean_sq = lax.optimization_barrier(jnp.mean(values * values, axis=-1, keepdims=True))
    return values * lax.rsqrt(mean_sq + epsilon) * gain

def rotary_embed(values, token_positions):
    half_dim = values.shape[-1] // 2
    frequencies = 10000.0 ** (-jnp.arange(half_dim, dtype=jnp.float32) / half_dim)
    angles = token_positions.astype(jnp.float32)[:, None] * frequencies[None, :]
    cosine = jnp.cos(angles)[:, None, :]
    sine_part = jnp.sin(angles)[:, None, :]
    first_half = values[..., :half_dim]
    second_half = values[..., half_dim:]
    return jnp.concatenate([first_half * cosine - second_half * sine_part, second_half * cosine + first_half * sine_part], axis=-1)

def stored_rows(values):
    return lax.optimization_barrier(values.astype(jnp.bfloat16)).astype(jnp.float32)

def reference(tokens, pre_gain, w_query, key_weight, value_weight, query_norm_gain, key_gain, w_out, post_gain):
    query_group_size = QUERY_HEADS // KEY_VALUE_HEADS
    group_cols = QUERY_HEADS * HEAD_SIZE // N_FSDP

    def one_document(doc_tokens):
        document_length = doc_tokens.shape[0]
        token_positions = jnp.arange(document_length, dtype=jnp.int32)
        normalized_rows = root_mean_norm(doc_tokens.astype(jnp.float32), pre_gain).astype(jnp.bfloat16)
        query_rows = jnp.dot(normalized_rows, w_query, preferred_element_type=jnp.float32).reshape(document_length, QUERY_HEADS, HEAD_SIZE)
        key_portion = jnp.dot(normalized_rows, key_weight, preferred_element_type=jnp.float32).reshape(document_length, KEY_VALUE_HEADS, HEAD_SIZE)
        value_portion = jnp.dot(normalized_rows, value_weight, preferred_element_type=jnp.float32).reshape(document_length, KEY_VALUE_HEADS, HEAD_SIZE)
        query_rows = stored_rows(rotary_embed(root_mean_norm(query_rows, query_norm_gain), token_positions)).reshape(document_length, KEY_VALUE_HEADS, query_group_size, HEAD_SIZE)
        key_portion = stored_rows(rotary_embed(root_mean_norm(key_portion, key_gain), token_positions))
        value_portion = stored_rows(value_portion)
        allowed = (token_positions[None, :] <= token_positions[:, None]) & (token_positions[:, None] - token_positions[None, :] < WINDOW)

        def single_head(head_index):
            q_head = query_rows[:, head_index]
            k_head = key_portion[:, head_index]
            v_head = value_portion[:, head_index]
            scores = jnp.einsum('qgc,kc->gqk', q_head, k_head) * score_scale
            unnorm = jnp.where(allowed[None], jnp.exp(scores), 0.0)
            totals = lax.optimization_barrier(jnp.sum(unnorm, axis=-1, keepdims=True))
            weights = stored_rows(unnorm / totals)
            return jnp.einsum('gqk,kc->qgc', weights, v_head).astype(jnp.bfloat16)
        head_outputs = lax.map(single_head, jnp.arange(KEY_VALUE_HEADS, dtype=jnp.int32))
        attended = jnp.transpose(head_outputs, (1, 0, 2, 3)).reshape(document_length, QUERY_HEADS * HEAD_SIZE)
        summed = jnp.zeros((document_length, MODEL_WIDTH), jnp.float32)
        for group_part in range(N_FSDP):
            lower = group_part * group_cols
            product = jnp.dot(attended[:, lower:lower + group_cols], w_out[lower:lower + group_cols], preferred_element_type=jnp.float32)
            summed = summed + stored_rows(product)
        return (doc_tokens.astype(jnp.float32) + root_mean_norm(summed, post_gain)).astype(jnp.bfloat16)
    return lax.map(one_document, tokens)
```

```python
import functools
import math

import jax
import jax.numpy as jnp
from jax import lax
from jax.experimental import pallas as pl
from jax.experimental.pallas import tpu as pltpu
from jax.sharding import PartitionSpec as P

epsilon = 1e-06
score_scale = 168.0 ** (-0.5)
window = 1024
vmem_limit = 58_000_000
MESH = pl.DeviceIdType.MESH
halves_of = ((0, 0), (1, 2), (2, 1), (3, 3))


def column_step(total, limit):
    step = 128
    for count in range(1, limit // 128 + 1):
        if total % (count * 128) == 0:
            step = count * 128
    return step


def layer_kernel(
    n_ctx, reach, q_heads, kv_heads, head, o_step,
    tok_hbm, wq_hbm, wk_hbm, wv_hbm, wo_hbm, pre_hbm, post_hbm, qg_hbm, kg_hbm,
    out_ref,
    w, wo, nb, nrm, raw, q, kv, att, pb, rx, ry, dg, small, gains, pre, post, cos, sin, accs, sums,
    load_sem, ag_s, ag_r, un_s, un_r, dc_s, dc_r, dr_s, dr_r, cb_s, cb_r, z_s, z_r, b_s, b_r, z_ready,
):
    f = lax.axis_index("fsdp")
    c = lax.axis_index("ctx")
    quarter, features = nb.shape[3:]
    half, rows = 2 * quarter, 4 * quarter
    z = c // 2
    p = c % 2
    nz = n_ctx // 2
    x_to = {"fsdp": f + 1 - 2 * (f % 2)}
    y_to = {"fsdp": (f + 2) % 4}
    sib = {"ctx": c + 1 - 2 * p}

    def ahead(step):
        return {"ctx": lax.rem(c + 2 * step, n_ctx)}, z + step < nz

    def behind(step):
        return {"ctx": lax.rem(c + n_ctx - 2 * step, n_ctx)}, z >= step

    direct = [step for step in (1, 3) if step <= reach]
    qw, kw = q_heads * head, kv_heads * head
    group = q_heads // kv_heads

    barrier = pltpu.get_barrier_semaphore()
    for to in (x_to, y_to, sib):
        pl.semaphore_signal(barrier, inc=1, device_id=to, device_id_type=MESH)
    peers, readers = 3, 0
    for step in direct:
        to, there = ahead(step)
        pl.when(there)(functools.partial(
            pl.semaphore_signal, barrier, inc=1, device_id=to, device_id_type=MESH
        ))
        peers = peers + jnp.clip(z - step + 1, 0, 1)
        readers = readers + jnp.clip(nz - z - step, 0, 1)

    def load(i, src, dst):
        return pltpu.make_async_copy(src, dst, load_sem.at[i])

    tok_load = load(0, tok_hbm, nb.at[0])
    small_loads = [
        load(1, pre_hbm, small.at[0]), load(2, post_hbm, small.at[1]),
        load(3, qg_hbm, gains.at[0]), load(4, kg_hbm, gains.at[1]),
    ]
    cut = features // 2
    w_loads = []
    for j, (src, lo, wide) in enumerate(((wk_hbm, qw, kw), (wv_hbm, qw + kw, kw), (wq_hbm, 0, qw))):
        for part in range(2):
            rs = pl.ds(part * cut, cut)
            w_loads.append(load(5 + 2 * j + part, src.at[rs], w.at[rs, pl.ds(lo, wide)]))
    wo_load = load(11, wo_hbm, wo)
    for d in [tok_load] + small_loads + w_loads + [wo_load]:
        d.start()

    def remote(src, dst, s, r, to):
        return pltpu.make_async_remote_copy(
            src_ref=src, dst_ref=dst, send_sem=s, recv_sem=r, device_id=to, device_id_type=MESH
        )

    def ag(link, k):
        part, h = k // 2, k % 2
        a = (link, 1 - link, 1 - link)[part]
        src = tok_hbm.at[a, h] if part < 2 else nb.at[1, a, h]
        return remote(src, nb.at[part + 1, a, h], ag_s.at[link, k], ag_r.at[link, k], (x_to, y_to)[link])

    pl.semaphore_wait(barrier, peers)
    for k in range(4):
        for link in range(2):
            ag(link, k).start()
    for step in direct:
        to, there = behind(step)
        pl.when(there)(functools.partial(
            pl.semaphore_signal, z_ready, inc=1, device_id=to, device_id_type=MESH
        ))

    r = lax.broadcasted_iota(jnp.int32, (rows, head), 0)
    lane = lax.broadcasted_iota(jnp.int32, (rows, head), 1)
    at_row = c * rows + (r // quarter) % 2 * half + r // half * quarter + r % quarter
    which = (lane % (head // 2)).astype(jnp.float32)
    angles = at_row.astype(jnp.float32) * jnp.exp(which * (-math.log(10000.0) / (head // 2)))
    cos[...] = jnp.cos(angles)
    sin[...] = jnp.where(lane < head // 2, -1.0, 1.0) * jnp.sin(angles)

    for d in small_loads:
        d.wait()
    for wide, i in ((pre, 0), (post, 1)):
        wide[...] = jnp.concatenate([small[i, k : k + 1, :] for k in range(small.shape[1])], axis=1)

    def norm(u, h):
        def body(i, carry):
            a, at = i // (quarter // 16), pl.ds(pl.multiple_of(i % (quarter // 16) * 16, 16), 16)
            v = nb[u, a, h, at, :].astype(jnp.float32)
            mean_sq = jnp.mean(v * v, axis=-1, keepdims=True)
            to = pl.ds(pl.multiple_of(h * half + i * 16, 16), 16)
            nrm[to, :] = (v * lax.rsqrt(mean_sq + epsilon) * pre[...]).astype(jnp.bfloat16)
            return carry

        lax.fori_loop(0, half // 16, body, 0)

    def z_copy(u, h, dz, step):
        return remote(
            kv.at[u, dz, p, :, h], kv.at[u, dz + step, p, :, h],
            z_s.at[u, h, dz + step], z_r.at[u, h, dz + step], ahead(step)[0],
        )

    def b_copy(u, h, dz):
        return remote(kv.at[u, dz, p, :, h], kv.at[u, dz, p, :, h], b_s.at[u, h, dz], b_r.at[u, h, dz], sib)

    def kv_arrived(u, h, dz):
        at = kv.at[u, dz, p, :, h]
        return remote(at, at, z_s.at[u, h, dz], z_r.at[u, h, dz], behind(1)[0])

    def kv_paired(u, h, dz):
        at = kv.at[u, dz, 1 - p, :, h]
        return remote(at, at, b_s.at[u, h, dz], b_r.at[u, h, dz], sib)

    def own_copies(u, h, act):
        for step in direct:
            @pl.when(ahead(step)[1])
            def _():
                act(z_copy(u, h, 0, step))

        @pl.when(p == 0)
        def _():
            act(b_copy(u, h, 0))

    def send_own(u, h):
        own_copies(u, h, lambda d: d.start())

    def passed_copies(u, h, dz, act):
        if dz in direct and dz + 1 <= reach:
            @pl.when(ahead(1)[1])
            def _():
                act(z_copy(u, h, dz, 1))

        act(b_copy(u, h, dz))

    def relay(u, h, dz):
        if dz > reach:
            return

        @pl.when(z >= dz)
        def _():
            kv_arrived(u, h, dz).wait_recv()
            passed_copies(u, h, dz, lambda d: d.start())

    def relay_rest(u, h):
        for dz in range(2, reach + 1):
            relay(u, h, dz)

    def wait_pairs(u):
        for h in range(2):
            @pl.when(p == 1)
            def _():
                kv_paired(u, h, 0).wait_recv()

            for dz in range(1, reach + 1):
                @pl.when(z >= dz)
                def _():
                    kv_paired(u, h, dz).wait_recv()

    k_step = column_step(2 * kw, 256)
    q_step = column_step(qw, 256)

    def columns_of(lo, size, first, count, step):
        def columns(j, carry):
            at = pl.ds(pl.multiple_of(first + j * step, 128), step)
            raw[lo : lo + size, at] = jnp.dot(nrm[lo : lo + size, :], w[:, at], preferred_element_type=jnp.float32)
            return carry

        lax.fori_loop(0, count // step, columns, 0)

    def rotated(lo, size, col, gain):
        v = raw[lo : lo + size, col : col + head]
        mean_sq = jnp.mean(v * v, axis=-1, keepdims=True)
        v = v * lax.rsqrt(mean_sq + epsilon) * gain
        v = v * cos[lo : lo + size, :] + pltpu.roll(v, head // 2, 1) * sin[lo : lo + size, :]
        return v.astype(jnp.bfloat16)

    def project_keys(u, h):
        lo = h * half
        columns_of(lo, half, qw, 2 * kw, k_step)
        for g in range(kv_heads):
            keys = rotated(lo, half, qw + g * head, gains[1])
            for a in range(2):
                kv[u, 0, p, a, h, :, g * head : (g + 1) * head] = keys[a * quarter : (a + 1) * quarter]
        for a in range(2):
            at = slice(lo + a * quarter, lo + (a + 1) * quarter)
            kv[u, 0, p, a, h, :, kw:] = raw[at, qw + kw :].astype(jnp.bfloat16)

    def project_queries(u):
        columns_of(0, rows, 0, qw, q_step)
        for g in range(q_heads):
            found = rotated(0, rows, g * head, gains[0])
            for h in range(2):
                for a in range(2):
                    to, at = a * half + h * quarter, (2 * h + a) * quarter
                    q[u, to : to + quarter, g * head : (g + 1) * head] = found[at : at + quarter]

    def merged(parts):
        return jnp.concatenate(parts, axis=0)

    def attend(u):
        own, other = halves_of[u], halves_of[(0, 2, 1, 3)[u]]
        spans = [(0, rows, own)] if own == other else [(0, half, own), (half, half, other)]
        streams = [
            (i * kv_heads + g, g, lo, size, units)
            for i, (lo, size, units) in enumerate(spans) for g in range(kv_heads)
        ]

        def places(lo, size):
            qi = lax.broadcasted_iota(jnp.int32, (group, size, rows), 1).reshape(group * size, rows) + lo
            return qi, lax.broadcasted_iota(jnp.int32, (group * size, rows), 1)

        def block(units, dz, par, cols):
            return merged([
                kv[units[a], dz, par, a, h, :, cols] for a in range(2) for h in range(2)
            ])

        def step(dz, pars, mask, first=False):
            for n, g, lo, size, units in streams:
                kc = slice(g * head, (g + 1) * head)
                vc = slice(kw + g * head, kw + (g + 1) * head)
                at = slice(0, group * size)
                queries = merged([
                    q[u, lo : lo + size, h * head : (h + 1) * head] for h in range(g * group, (g + 1) * group)
                ])
                keys = merged([block(units, dz, par, kc) for par in pars])
                values = merged([block(units, dz, par, vc) for par in pars])
                s = lax.dot_general(queries, keys, (((1,), (1,)), ((), ())), preferred_element_type=jnp.float32)
                e = jnp.exp(s * score_scale)
                if mask is not None:
                    e = jnp.where(mask(lo, size), e, 0.0)
                total = sum(e[:, i * rows : (i + 1) * rows] for i in range(len(pars)))
                acc = jnp.dot(e.astype(jnp.bfloat16), values, preferred_element_type=jnp.float32)
                if first:
                    sums[n, at], accs[n, at] = total, acc
                else:
                    sums[n, at] += total
                    accs[n, at] += acc

        def causal(lo, size):
            qi, kj = places(lo, size)
            return kj <= qi

        step(0, [p], causal, True)

        def beside(_, carry):
            step(0, [0], None)
            return carry

        def earlier(dz, carry):
            def near(lo, size):
                qi, kj = places(lo, size)
                apart = (p + 2 * dz) * rows + qi - kj
                return jnp.concatenate([apart, apart - rows], axis=1) < window

            step(dz, [0, 1], near if n_ctx * rows > window else None)
            return carry

        lax.fori_loop(0, p, beside, 0)
        lax.fori_loop(1, jnp.minimum(z, reach) + 1, earlier, 0)
        for n, g, lo, size, _ in streams:
            at = slice(0, group * size)
            o = (accs[n, at] / jnp.sum(sums[n, at], axis=-1, keepdims=True)).astype(jnp.bfloat16)
            for i in range(group):
                h = g * group + i
                att[u, lo : lo + size, h * head : (h + 1) * head] = o[i * size : (i + 1) * size]

    blocks = features // o_step

    def output(u, send=None):
        def columns(j, carry):
            at = pl.ds(pl.multiple_of(j * o_step, o_step), o_step)
            pb[u, :, at] = jnp.dot(att[u], wo[:, at], preferred_element_type=jnp.float32).astype(jnp.bfloat16)
            if send is not None:
                pl.when(j > 0)(lambda: send(j - 1))
            return carry

        lax.fori_loop(0, blocks, columns, 0)
        if send is not None:
            send(blocks - 1)

    def unit_copy(link, j):
        at = (pl.ds(link * half, half), pl.ds(pl.multiple_of(j * o_step, o_step), o_step))
        return remote(
            pb.at[(1, *at)], (rx, ry)[link].at[at], un_s.at[link, j], un_r.at[link, j], (x_to, y_to)[link]
        )

    def far_columns(link, j):
        at = (pl.ds(link * half, quarter), pl.ds(pl.multiple_of(j * o_step, o_step), o_step))
        return remote(pb.at[(3, *at)], dg.at[at], dc_s.at[link, j], dc_r.at[link, j], (x_to, y_to)[link])

    def far_rows(link, i):
        at = pl.ds(link * half + quarter + i * 16, 16)
        return remote(pb.at[3, at], dg.at[at], dr_s.at[link, i], dr_r.at[link, i], (x_to, y_to)[link])

    def sum_copy(link, i):
        at = pl.ds((1 - link) * half + i * 16, 16)
        return remote(pb.at[2, at], (rx, ry)[link].at[at], cb_s.at[link, i], cb_r.at[link, i], (x_to, y_to)[link])

    def both(copy, i, act="start"):
        for link in range(2):
            getattr(copy(link, i), act)()

    def every(copy, count, act):
        def body(j, carry):
            both(copy, j, act)
            return carry

        lax.fori_loop(0, count, body, 0)

    def add_rows(at):
        pb[2, at, :] = (pb[2, at, :].astype(jnp.float32) + dg[at, :].astype(jnp.float32)).astype(jnp.bfloat16)

    def arrive(u, h):
        both(ag, 2 * (u - 1) + h, "wait_recv")
        if u == 1:
            both(ag, 4 + h)
        norm(u, h)
        project_keys(u, h)

    tok_load.wait()
    norm(0, 0)
    norm(0, 1)
    for d in w_loads[:4]:
        d.wait()
    project_keys(0, 0)
    project_keys(0, 1)
    for d in w_loads[4:]:
        d.wait()
    project_queries(0)
    arrive(1, 0)
    pl.when(readers > 0)(lambda: pl.semaphore_wait(z_ready, readers))
    send_own(1, 0)
    arrive(1, 1)
    send_own(1, 1)
    relay(1, 0, 1)
    project_queries(1)
    relay(1, 1, 1)
    arrive(2, 0)
    send_own(2, 0)
    relay_rest(1, 0)
    wo_load.wait()
    arrive(2, 1)
    send_own(2, 1)
    relay(2, 0, 1)
    relay_rest(1, 1)
    project_queries(2)
    relay(2, 1, 1)
    relay_rest(2, 0)
    arrive(3, 0)
    send_own(3, 0)
    relay_rest(2, 1)
    wait_pairs(1)
    wait_pairs(2)
    attend(1)
    output(1, lambda j: both(unit_copy, j))
    arrive(3, 1)
    send_own(3, 1)
    relay(3, 0, 1)
    project_queries(3)
    attend(2)
    relay(3, 1, 1)
    relay_rest(3, 0)
    send_own(0, 0)
    send_own(0, 1)
    output(2)
    relay_rest(3, 1)
    wait_pairs(3)
    attend(3)
    output(3, lambda j: both(far_columns, j))
    for i in range(quarter // 16):
        both(far_rows, i)
    relay(0, 0, 1)
    relay(0, 1, 1)

    every(far_columns, blocks, "wait_recv")
    tiles = half // 16
    for i in range(tiles):
        if i >= tiles // 2:
            both(far_rows, i - tiles // 2, "wait_recv")
        for a in range(2):
            add_rows(pl.ds(a * half + i * 16, 16))
        both(sum_copy, i)
    relay_rest(0, 0)
    relay_rest(0, 1)
    wait_pairs(0)
    attend(0)
    output(0)

    every(unit_copy, blocks, "wait_recv")
    for i in range(tiles):
        both(sum_copy, i, "wait_recv")
        for a in range(2):
            at = pl.ds(a * half + i * 16, 16)
            summed = pb[0, at, :].astype(jnp.float32) + rx[at, :].astype(jnp.float32) + ry[at, :].astype(jnp.float32)
            mean_sq = jnp.mean(summed * summed, axis=-1, keepdims=True)
            normed = summed * lax.rsqrt(mean_sq + epsilon) * post[...]
            mine = nb[0, a, i * 16 // quarter, pl.ds(i * 16 % quarter, 16), :].astype(jnp.float32)
            out_ref[at, :] = (mine + normed).astype(jnp.bfloat16)

    for k in range(6):
        both(ag, k, "wait_send")
    every(unit_copy, blocks, "wait_send")
    every(far_columns, blocks, "wait_send")
    for i in range(quarter // 16):
        both(far_rows, i, "wait_send")
    for i in range(tiles):
        both(sum_copy, i, "wait_send")
    for u in range(4):
        for h in range(2):
            own_copies(u, h, lambda d: d.wait_send())
            for dz in range(1, reach + 1):
                @pl.when(z >= dz)
                def _():
                    passed_copies(u, h, dz, lambda d: d.wait_send())


def per_device(
    n_ctx, tokens, pre_gain, w_query, key_weight, value_weight, query_norm_gain, key_gain, w_out, post_gain
):
    _, rows, features = tokens.shape
    head = query_norm_gain.shape[0]
    qw, kw = w_query.shape[1], key_weight.shape[1]
    reach = min(n_ctx // 2 - 1, -(-window // (2 * rows)))
    o_step = column_step(features, 768)
    blocks, tiles, quarter = features // o_step, rows // 32, rows // 4
    any_spec = pl.BlockSpec(memory_space=pl.ANY)
    bf16, f32 = jnp.bfloat16, jnp.float32
    dma = pltpu.SemaphoreType.DMA
    out = pl.pallas_call(
        functools.partial(layer_kernel, n_ctx, reach, qw // head, kw // head, head, o_step),
        out_shape=pltpu.VMEM((rows, features), bf16),
        in_specs=[any_spec] * 9,
        out_specs=pl.BlockSpec(memory_space=pltpu.VMEM),
        scratch_shapes=[
            pltpu.VMEM((features, qw + 2 * kw), bf16),
            pltpu.VMEM((qw, features), bf16),
            pltpu.VMEM((4, 2, 2, quarter, features), bf16),
            pltpu.VMEM((rows, features), bf16),
            pltpu.VMEM((rows, qw + 2 * kw), f32),
            pltpu.VMEM((4, rows, qw), bf16),
            pltpu.VMEM((4, reach + 1, 2, 2, 2, quarter, 2 * kw), bf16),
            pltpu.VMEM((4, rows, qw), bf16),
            pltpu.VMEM((4, rows, features), bf16),
            pltpu.VMEM((rows, features), bf16),
            pltpu.VMEM((rows, features), bf16),
            pltpu.VMEM((rows, features), bf16),
            pltpu.VMEM((2, features // 128, 128), f32),
            pltpu.VMEM((2, 1, head), f32),
            pltpu.VMEM((1, features), f32),
            pltpu.VMEM((1, features), f32),
            pltpu.VMEM((rows, head), f32),
            pltpu.VMEM((rows, head), f32),
            pltpu.VMEM((2 * kw // head, qw // kw * rows, head), f32),
            pltpu.VMEM((2 * kw // head, qw // kw * rows, rows), f32),
            dma((12,)), dma((2, 6)), dma((2, 6)),
            dma((2, blocks)), dma((2, blocks)), dma((2, blocks)), dma((2, blocks)),
            dma((2, tiles // 2)), dma((2, tiles // 2)), dma((2, tiles)), dma((2, tiles)),
            dma((4, 2, reach + 1)), dma((4, 2, reach + 1)), dma((4, 2, reach + 1)), dma((4, 2, reach + 1)),
            pltpu.SemaphoreType.REGULAR,
        ],
        compiler_params=pltpu.CompilerParams(
            collective_id=0, has_side_effects=True, vmem_limit_bytes=vmem_limit
        ),
    )(
        tokens.reshape(2, 2, quarter, features), w_query, key_weight, value_weight, w_out,
        pre_gain.reshape(-1, 128), post_gain.reshape(-1, 128), query_norm_gain[None], key_gain[None],
    )
    return out[None]


def solution(mesh):
    return jax.shard_map(
        functools.partial(per_device, mesh.shape["ctx"]),
        mesh=mesh,
        in_specs=(
            P("fsdp", "ctx", None),
            P(),
            P(None, "fsdp"),
            P(None, "fsdp"),
            P(None, "fsdp"),
            P(),
            P(),
            P("fsdp", None),
            P(),
        ),
        out_specs=P("fsdp", "ctx", None),
        check_vma=False,
    )
```

```python
import functools
import math

import jax
import jax.numpy as jnp
from jax import lax
from jax.experimental import pallas as pl
from jax.experimental.pallas import tpu as pltpu
from jax.sharding import PartitionSpec as P

epsilon = 1e-06
score_scale = 168.0 ** (-0.5)
window = 1024
vmem_limit = 58_000_000
MESH = pl.DeviceIdType.MESH
halves_of = ((0, 0), (1, 2), (2, 1), (3, 3))


def column_step(total, limit):
    step = 128
    for count in range(1, limit // 128 + 1):
        if total % (count * 128) == 0:
            step = count * 128
    return step


def layer_kernel(
    n_ctx, reach, q_heads, kv_heads, head, o_step,
    tok_hbm, wq_hbm, wk_hbm, wv_hbm, wo_hbm, pre_hbm, post_hbm, qg_hbm, kg_hbm,
    out_ref,
    w, wo, nb, nrm, raw, q, kv, att, pb, rx, ry, dg, small, gains, pre, post, cos, sin, accs, sums,
    load_sem, ag_s, ag_r, un_s, un_r, dc_s, dc_r, dr_s, dr_r, cb_s, cb_r, z_s, z_r, b_s, b_r, z_ready,
):
    f = lax.axis_index("fsdp")
    c = lax.axis_index("ctx")
    quarter, features = nb.shape[3:]
    half, rows = 2 * quarter, 4 * quarter
    z = c // 2
    p = c % 2
    nz = n_ctx // 2
    x_to = {"fsdp": f + 1 - 2 * (f % 2)}
    y_to = {"fsdp": (f + 2) % 4}
    sib = {"ctx": c + 1 - 2 * p}

    def ahead(step):
        return {"ctx": lax.rem(c + 2 * step, n_ctx)}, z + step < nz

    def behind(step):
        return {"ctx": lax.rem(c + n_ctx - 2 * step, n_ctx)}, z >= step

    direct = [step for step in (1, 3) if step <= reach]
    qw, kw = q_heads * head, kv_heads * head
    group = q_heads // kv_heads

    barrier = pltpu.get_barrier_semaphore()
    for to in (x_to, y_to, sib):
        pl.semaphore_signal(barrier, inc=1, device_id=to, device_id_type=MESH)
    peers, readers = 3, 0
    for step in direct:
        to, there = ahead(step)
        pl.when(there)(functools.partial(
            pl.semaphore_signal, barrier, inc=1, device_id=to, device_id_type=MESH
        ))
        peers = peers + jnp.clip(z - step + 1, 0, 1)
        readers = readers + jnp.clip(nz - z - step, 0, 1)

    def load(i, src, dst):
        return pltpu.make_async_copy(src, dst, load_sem.at[i])

    tok_load = load(0, tok_hbm, nb.at[0])
    small_loads = [
        load(1, pre_hbm, small.at[0]), load(2, post_hbm, small.at[1]),
        load(3, qg_hbm, gains.at[0]), load(4, kg_hbm, gains.at[1]),
    ]
    cut = features // 2
    w_loads = []
    for j, (src, lo, wide) in enumerate(((wk_hbm, qw, kw), (wv_hbm, qw + kw, kw), (wq_hbm, 0, qw))):
        for part in range(2):
            rs = pl.ds(part * cut, cut)
            w_loads.append(load(5 + 2 * j + part, src.at[rs], w.at[rs, pl.ds(lo, wide)]))
    wo_load = load(11, wo_hbm, wo)
    for d in [tok_load] + small_loads + w_loads + [wo_load]:
        d.start()

    def remote(src, dst, s, r, to):
        return pltpu.make_async_remote_copy(
            src_ref=src, dst_ref=dst, send_sem=s, recv_sem=r, device_id=to, device_id_type=MESH
        )

    def ag(link, k):
        part, h = k // 2, k % 2
        a = (link, 1 - link, 1 - link)[part]
        src = tok_hbm.at[a, h] if part < 2 else nb.at[1, a, h]
        return remote(src, nb.at[part + 1, a, h], ag_s.at[link, k], ag_r.at[link, k], (x_to, y_to)[link])

    pl.semaphore_wait(barrier, peers)
    for k in range(4):
        for link in range(2):
            ag(link, k).start()
    for step in direct:
        to, there = behind(step)
        pl.when(there)(functools.partial(
            pl.semaphore_signal, z_ready, inc=1, device_id=to, device_id_type=MESH
        ))

    r = lax.broadcasted_iota(jnp.int32, (rows, head), 0)
    lane = lax.broadcasted_iota(jnp.int32, (rows, head), 1)
    at_row = c * rows + (r // quarter) % 2 * half + r // half * quarter + r % quarter
    which = (lane % (head // 2)).astype(jnp.float32)
    angles = at_row.astype(jnp.float32) * jnp.exp(which * (-math.log(10000.0) / (head // 2)))
    cos[...] = jnp.cos(angles)
    sin[...] = jnp.where(lane < head // 2, -1.0, 1.0) * jnp.sin(angles)

    for d in small_loads:
        d.wait()
    for wide, i in ((pre, 0), (post, 1)):
        wide[...] = jnp.concatenate([small[i, k : k + 1, :] for k in range(small.shape[1])], axis=1)

    def norm(u, h):
        def body(i, carry):
            a, at = i // (quarter // 16), pl.ds(pl.multiple_of(i % (quarter // 16) * 16, 16), 16)
            v = nb[u, a, h, at, :].astype(jnp.float32)
            mean_sq = jnp.mean(v * v, axis=-1, keepdims=True)
            to = pl.ds(pl.multiple_of(h * half + i * 16, 16), 16)
            nrm[to, :] = (v * lax.rsqrt(mean_sq + epsilon) * pre[...]).astype(jnp.bfloat16)
            return carry

        lax.fori_loop(0, half // 16, body, 0)

    def z_copy(u, h, dz, step):
        return remote(
            kv.at[u, dz, p, :, h], kv.at[u, dz + step, p, :, h],
            z_s.at[u, h, dz + step], z_r.at[u, h, dz + step], ahead(step)[0],
        )

    def b_copy(u, h, dz):
        return remote(kv.at[u, dz, p, :, h], kv.at[u, dz, p, :, h], b_s.at[u, h, dz], b_r.at[u, h, dz], sib)

    def kv_arrived(u, h, dz):
        at = kv.at[u, dz, p, :, h]
        return remote(at, at, z_s.at[u, h, dz], z_r.at[u, h, dz], behind(1)[0])

    def kv_paired(u, h, dz):
        at = kv.at[u, dz, 1 - p, :, h]
        return remote(at, at, b_s.at[u, h, dz], b_r.at[u, h, dz], sib)

    def own_copies(u, h, act):
        for step in direct:
            @pl.when(ahead(step)[1])
            def _():
                act(z_copy(u, h, 0, step))

        @pl.when(p == 0)
        def _():
            act(b_copy(u, h, 0))

    def send_own(u, h):
        own_copies(u, h, lambda d: d.start())

    def passed_copies(u, h, dz, act):
        if dz in direct and dz + 1 <= reach:
            @pl.when(ahead(1)[1])
            def _():
                act(z_copy(u, h, dz, 1))

        act(b_copy(u, h, dz))

    def relay(u, h, dz):
        if dz > reach:
            return

        @pl.when(z >= dz)
        def _():
            kv_arrived(u, h, dz).wait_recv()
            passed_copies(u, h, dz, lambda d: d.start())

    farthest = jnp.minimum(z, reach)

    def share(units, dz):
        for u in units:
            for h in range(2):
                kv_arrived(u, h, dz).wait_recv()
                for step in direct:
                    if step > 1 and step + 1 <= reach:
                        pl.when((dz == step) & ahead(1)[1])(z_copy(u, h, step, 1).start)
                b_copy(u, h, dz).start()

    def wait_pairs(units, dz):
        for u in units:
            for h in range(2):
                kv_paired(u, h, dz).wait_recv()

    k_step = column_step(2 * kw, 256)
    q_step = column_step(qw, 256)

    def columns_of(lo, size, first, count, step):
        def columns(j, carry):
            at = pl.ds(pl.multiple_of(first + j * step, 128), step)
            raw[lo : lo + size, at] = jnp.dot(nrm[lo : lo + size, :], w[:, at], preferred_element_type=jnp.float32)
            return carry

        lax.fori_loop(0, count // step, columns, 0)

    def rotated(lo, size, col, gain):
        v = raw[lo : lo + size, col : col + head]
        mean_sq = jnp.mean(v * v, axis=-1, keepdims=True)
        v = v * lax.rsqrt(mean_sq + epsilon) * gain
        v = v * cos[lo : lo + size, :] + pltpu.roll(v, head // 2, 1) * sin[lo : lo + size, :]
        return v.astype(jnp.bfloat16)

    def project_keys(u, h):
        lo = h * half
        columns_of(lo, half, qw, 2 * kw, k_step)
        for g in range(kv_heads):
            keys = rotated(lo, half, qw + g * head, gains[1])
            for a in range(2):
                kv[u, 0, p, a, h, :, g * head : (g + 1) * head] = keys[a * quarter : (a + 1) * quarter]
        for a in range(2):
            at = slice(lo + a * quarter, lo + (a + 1) * quarter)
            kv[u, 0, p, a, h, :, kw:] = raw[at, qw + kw :].astype(jnp.bfloat16)

    def project_queries(u):
        columns_of(0, rows, 0, qw, q_step)
        for g in range(q_heads):
            found = rotated(0, rows, g * head, gains[0])
            for h in range(2):
                for a in range(2):
                    to, at = a * half + h * quarter, (2 * h + a) * quarter
                    q[u, to : to + quarter, g * head : (g + 1) * head] = found[at : at + quarter]

    def merged(parts):
        return jnp.concatenate(parts, axis=0)

    def attention(u, fresh):
        own, other = halves_of[u], halves_of[(0, 2, 1, 3)[u]]
        spans = [(0, rows, own)] if own == other else [(0, half, own), (half, half, other)]
        streams = [
            (i * kv_heads + g, g, lo, size, units)
            for i, (lo, size, units) in enumerate(spans) for g in range(kv_heads)
        ]

        def places(lo, size):
            qi = lax.broadcasted_iota(jnp.int32, (group, size, rows), 1).reshape(group * size, rows) + lo
            return qi, lax.broadcasted_iota(jnp.int32, (group * size, rows), 1)

        def block(units, dz, par, cols):
            return merged([
                kv[units[a], dz, par, a, h, :, cols] for a in range(2) for h in range(2)
            ])

        def step(dz, pars, mask, first=False):
            for n, g, lo, size, units in streams:
                kc = slice(g * head, (g + 1) * head)
                vc = slice(kw + g * head, kw + (g + 1) * head)
                at = slice(0, group * size)
                queries = merged([
                    q[u, lo : lo + size, h * head : (h + 1) * head] for h in range(g * group, (g + 1) * group)
                ])
                keys = merged([block(units, dz, par, kc) for par in pars])
                values = merged([block(units, dz, par, vc) for par in pars])
                s = lax.dot_general(queries, keys, (((1,), (1,)), ((), ())), preferred_element_type=jnp.float32)
                e = jnp.exp(s * score_scale)
                if mask is not None:
                    e = jnp.where(mask(lo, size), e, 0.0)
                total = sum(e[:, i * rows : (i + 1) * rows] for i in range(len(pars)))
                acc = jnp.dot(e.astype(jnp.bfloat16), values, preferred_element_type=jnp.float32)
                if first:
                    sums[n, at], accs[n, at] = total, acc
                else:
                    sums[n, at] += total
                    accs[n, at] += acc

        def causal(lo, size):
            qi, kj = places(lo, size)
            return kj <= qi

        def begin():
            step(0, [p], causal, True)

            def beside(_, carry):
                wait_pairs(fresh, 0)
                step(0, [0], None)
                return carry

            lax.fori_loop(0, p, beside, 0)

        def earlier(dz, carry):
            def near(lo, size):
                qi, kj = places(lo, size)
                apart = (p + 2 * dz) * rows + qi - kj
                return jnp.concatenate([apart, apart - rows], axis=1) < window

            pl.when(dz + 1 <= farthest)(lambda: share(fresh, dz + 1))
            wait_pairs(fresh, dz)
            step(dz, [0, 1], near if n_ctx * rows > window else None)
            return carry

        def complete():
            lax.fori_loop(1, farthest + 1, earlier, 0)
            for n, g, lo, size, _ in streams:
                at = slice(0, group * size)
                o = (accs[n, at] / jnp.sum(sums[n, at], axis=-1, keepdims=True)).astype(jnp.bfloat16)
                for i in range(group):
                    h = g * group + i
                    att[u, lo : lo + size, h * head : (h + 1) * head] = o[i * size : (i + 1) * size]

        return begin, complete

    def attend(u, fresh):
        for part in attention(u, fresh):
            part()

    blocks = features // o_step

    def output(u, send=None, first=0, last=blocks):
        def columns(j, carry):
            at = pl.ds(pl.multiple_of(j * o_step, o_step), o_step)
            pb[u, :, at] = jnp.dot(att[u], wo[:, at], preferred_element_type=jnp.float32).astype(jnp.bfloat16)
            if send is not None:
                pl.when(j > 0)(lambda: send(j - 1))
            return carry

        lax.fori_loop(first, last, columns, 0)
        if send is not None and last == blocks:
            send(blocks - 1)

    def unit_copy(link, j):
        at = (pl.ds(link * half, half), pl.ds(pl.multiple_of(j * o_step, o_step), o_step))
        return remote(
            pb.at[(1, *at)], (rx, ry)[link].at[at], un_s.at[link, j], un_r.at[link, j], (x_to, y_to)[link]
        )

    def far_columns(link, j):
        at = (pl.ds(link * half, quarter), pl.ds(pl.multiple_of(j * o_step, o_step), o_step))
        return remote(pb.at[(3, *at)], dg.at[at], dc_s.at[link, j], dc_r.at[link, j], (x_to, y_to)[link])

    def far_rows(link, i):
        at = pl.ds(link * half + quarter + i * 16, 16)
        return remote(pb.at[3, at], dg.at[at], dr_s.at[link, i], dr_r.at[link, i], (x_to, y_to)[link])

    def sum_copy(link, i):
        at = pl.ds((1 - link) * half + i * 16, 16)
        return remote(pb.at[2, at], (rx, ry)[link].at[at], cb_s.at[link, i], cb_r.at[link, i], (x_to, y_to)[link])

    def both(copy, i, act="start"):
        for link in range(2):
            getattr(copy(link, i), act)()

    def every(copy, count, act):
        def body(j, carry):
            both(copy, j, act)
            return carry

        lax.fori_loop(0, count, body, 0)

    def add_rows(at):
        pb[2, at, :] = (pb[2, at, :].astype(jnp.float32) + dg[at, :].astype(jnp.float32)).astype(jnp.bfloat16)

    def arrive(u, h, between=None):
        both(ag, 2 * (u - 1) + h, "wait_recv")
        if u == 1:
            both(ag, 4 + h)
        norm(u, h)
        if between is not None:
            between()
        project_keys(u, h)
        send_own(u, h)

    tok_load.wait()
    norm(0, 0)
    norm(0, 1)
    for d in w_loads[:4]:
        d.wait()
    project_keys(0, 0)
    pl.when(readers > 0)(lambda: pl.semaphore_wait(z_ready, readers))
    send_own(0, 0)
    project_keys(0, 1)
    for d in w_loads[4:]:
        d.wait()
    project_queries(0)
    arrive(1, 0)
    relay(0, 0, 1)
    arrive(1, 1)
    relay(1, 0, 1)
    project_queries(1)
    relay(1, 1, 1)
    arrive(2, 0)
    wo_load.wait()
    arrive(2, 1, lambda: relay(2, 0, 1))
    project_queries(2)
    begin, complete = attention(1, (1, 2))
    begin()
    relay(2, 1, 1)
    arrive(3, 0)
    complete()
    unit_send = lambda j: both(unit_copy, j)
    early = min(3, blocks)
    output(1, unit_send, 0, early)
    arrive(3, 1, lambda: relay(3, 0, 1))
    output(1, unit_send, early, blocks)
    attend(2, ())
    relay(3, 1, 1)
    send_own(0, 1)
    project_queries(3)
    attend(3, (3,))
    output(3, lambda j: both(far_columns, j))
    for i in range(quarter // 16):
        both(far_rows, i)
    relay(0, 1, 1)
    output(2)
    attend(0, (0,))

    every(far_columns, blocks, "wait_recv")
    tiles = half // 16
    for i in range(tiles):
        if i >= tiles // 2:
            both(far_rows, i - tiles // 2, "wait_recv")
        for a in range(2):
            add_rows(pl.ds(a * half + i * 16, 16))
        both(sum_copy, i)
    output(0)

    every(unit_copy, blocks, "wait_recv")
    for i in range(tiles):
        both(sum_copy, i, "wait_recv")
        for a in range(2):
            at = pl.ds(a * half + i * 16, 16)
            summed = pb[0, at, :].astype(jnp.float32) + rx[at, :].astype(jnp.float32) + ry[at, :].astype(jnp.float32)
            mean_sq = jnp.mean(summed * summed, axis=-1, keepdims=True)
            normed = summed * lax.rsqrt(mean_sq + epsilon) * post[...]
            mine = nb[0, a, i * 16 // quarter, pl.ds(i * 16 % quarter, 16), :].astype(jnp.float32)
            out_ref[at, :] = (mine + normed).astype(jnp.bfloat16)

    for k in range(6):
        both(ag, k, "wait_send")
    every(unit_copy, blocks, "wait_send")
    every(far_columns, blocks, "wait_send")
    for i in range(quarter // 16):
        both(far_rows, i, "wait_send")
    for i in range(tiles):
        both(sum_copy, i, "wait_send")
    for u in range(4):
        for h in range(2):
            own_copies(u, h, lambda d: d.wait_send())
            for dz in range(1, reach + 1):
                @pl.when(z >= dz)
                def _():
                    passed_copies(u, h, dz, lambda d: d.wait_send())


def per_device(
    n_ctx, tokens, pre_gain, w_query, key_weight, value_weight, query_norm_gain, key_gain, w_out, post_gain
):
    _, rows, features = tokens.shape
    head = query_norm_gain.shape[0]
    qw, kw = w_query.shape[1], key_weight.shape[1]
    reach = min(n_ctx // 2 - 1, -(-window // (2 * rows)))
    o_step = column_step(features, 768)
    blocks, tiles, quarter = features // o_step, rows // 32, rows // 4
    any_spec = pl.BlockSpec(memory_space=pl.ANY)
    bf16, f32 = jnp.bfloat16, jnp.float32
    dma = pltpu.SemaphoreType.DMA
    out = pl.pallas_call(
        functools.partial(layer_kernel, n_ctx, reach, qw // head, kw // head, head, o_step),
        out_shape=pltpu.VMEM((rows, features), bf16),
        in_specs=[any_spec] * 9,
        out_specs=pl.BlockSpec(memory_space=pltpu.VMEM),
        scratch_shapes=[
            pltpu.VMEM((features, qw + 2 * kw), bf16),
            pltpu.VMEM((qw, features), bf16),
            pltpu.VMEM((4, 2, 2, quarter, features), bf16),
            pltpu.VMEM((rows, features), bf16),
            pltpu.VMEM((rows, qw + 2 * kw), f32),
            pltpu.VMEM((4, rows, qw), bf16),
            pltpu.VMEM((4, reach + 1, 2, 2, 2, quarter, 2 * kw), bf16),
            pltpu.VMEM((4, rows, qw), bf16),
            pltpu.VMEM((4, rows, features), bf16),
            pltpu.VMEM((rows, features), bf16),
            pltpu.VMEM((rows, features), bf16),
            pltpu.VMEM((rows, features), bf16),
            pltpu.VMEM((2, features // 128, 128), f32),
            pltpu.VMEM((2, 1, head), f32),
            pltpu.VMEM((1, features), f32),
            pltpu.VMEM((1, features), f32),
            pltpu.VMEM((rows, head), f32),
            pltpu.VMEM((rows, head), f32),
            pltpu.VMEM((2 * kw // head, qw // kw * rows, head), f32),
            pltpu.VMEM((2 * kw // head, qw // kw * rows, rows), f32),
            dma((12,)), dma((2, 6)), dma((2, 6)),
            dma((2, blocks)), dma((2, blocks)), dma((2, blocks)), dma((2, blocks)),
            dma((2, tiles // 2)), dma((2, tiles // 2)), dma((2, tiles)), dma((2, tiles)),
            dma((4, 2, reach + 1)), dma((4, 2, reach + 1)), dma((4, 2, reach + 1)), dma((4, 2, reach + 1)),
            pltpu.SemaphoreType.REGULAR,
        ],
        compiler_params=pltpu.CompilerParams(
            collective_id=0, has_side_effects=True, vmem_limit_bytes=vmem_limit
        ),
    )(
        tokens.reshape(2, 2, quarter, features), w_query, key_weight, value_weight, w_out,
        pre_gain.reshape(-1, 128), post_gain.reshape(-1, 128), query_norm_gain[None], key_gain[None],
    )
    return out[None]


def solution(mesh):
    return jax.shard_map(
        functools.partial(per_device, mesh.shape["ctx"]),
        mesh=mesh,
        in_specs=(
            P("fsdp", "ctx", None),
            P(),
            P(None, "fsdp"),
            P(None, "fsdp"),
            P(None, "fsdp"),
            P(),
            P(),
            P("fsdp", None),
            P(),
        ),
        out_specs=P("fsdp", "ctx", None),
        check_vma=False,
    )
```

```python
import functools
import math

import jax
import jax.numpy as jnp
from jax import lax
from jax.experimental import pallas as pl
from jax.experimental.pallas import tpu as pltpu
from jax.sharding import PartitionSpec as P

epsilon = 1e-06
score_scale = 168.0 ** (-0.5)
window = 1024
vmem_limit = 58_000_000
MESH = pl.DeviceIdType.MESH
halves_of = ((0, 0), (1, 2), (2, 1), (3, 3))


def column_step(total, limit):
    step = 128
    for count in range(1, limit // 128 + 1):
        if total % (count * 128) == 0:
            step = count * 128
    return step


def layer_kernel(
    n_ctx, reach, q_heads, kv_heads, head, o_step, cuts,
    tok_hbm, wq_hbm, wk_hbm, wv_hbm, wo_hbm, pre_hbm, post_hbm, qg_hbm, kg_hbm,
    out_ref,
    w, wo, nb, nrm, raw, q, kv, att, pb, rx, ry, dg, small, gains, pre, post, cos, sin, accs, sums,
    load_sem, ag_s, ag_r, un_s, un_r, dc_s, dc_r, dr_s, dr_r, cb_s, cb_r, z_s, z_r, b_s, b_r, z_ready,
):
    f = lax.axis_index("fsdp")
    c = lax.axis_index("ctx")
    quarter, features = nb.shape[3:]
    half, rows = 2 * quarter, 4 * quarter
    z = c // 2
    p = c % 2
    nz = n_ctx // 2
    x_to = {"fsdp": f + 1 - 2 * (f % 2)}
    y_to = {"fsdp": (f + 2) % 4}
    sib = {"ctx": c + 1 - 2 * p}

    def ahead(step):
        return {"ctx": lax.rem(c + 2 * step, n_ctx)}, z + step < nz

    def behind(step):
        return {"ctx": lax.rem(c + n_ctx - 2 * step, n_ctx)}, z >= step

    direct = [step for step in (1, 3) if step <= reach]
    qw, kw = q_heads * head, kv_heads * head
    group = q_heads // kv_heads

    barrier = pltpu.get_barrier_semaphore()
    for to in (x_to, y_to, sib):
        pl.semaphore_signal(barrier, inc=1, device_id=to, device_id_type=MESH)
    peers, readers = 3, 0
    for step in direct:
        to, there = ahead(step)
        pl.when(there)(functools.partial(
            pl.semaphore_signal, barrier, inc=1, device_id=to, device_id_type=MESH
        ))
        peers = peers + jnp.clip(z - step + 1, 0, 1)
        readers = readers + jnp.clip(nz - z - step, 0, 1)

    def load(i, src, dst):
        return pltpu.make_async_copy(src, dst, load_sem.at[i])

    tok_load = load(0, tok_hbm, nb.at[0])
    small_loads = [
        load(1, pre_hbm, small.at[0]), load(2, post_hbm, small.at[1]),
        load(3, qg_hbm, gains.at[0]), load(4, kg_hbm, gains.at[1]),
    ]
    cut = features // 2
    w_loads = []
    for j, (src, lo, wide) in enumerate(((wk_hbm, qw, kw), (wv_hbm, qw + kw, kw), (wq_hbm, 0, qw))):
        for part in range(2):
            rs = pl.ds(part * cut, cut)
            w_loads.append(load(5 + 2 * j + part, src.at[rs], w.at[rs, pl.ds(lo, wide)]))
    wo_load = load(11, wo_hbm, wo)
    for d in [tok_load] + small_loads + w_loads + [wo_load]:
        d.start()

    def remote(src, dst, s, r, to):
        return pltpu.make_async_remote_copy(
            src_ref=src, dst_ref=dst, send_sem=s, recv_sem=r, device_id=to, device_id_type=MESH
        )

    def ag(link, k):
        part, h = k // 2, k % 2
        a = (link, 1 - link, 1 - link)[part]
        src = tok_hbm.at[a, h] if part < 2 else nb.at[1, a, h]
        return remote(src, nb.at[part + 1, a, h], ag_s.at[link, k], ag_r.at[link, k], (x_to, y_to)[link])

    pl.semaphore_wait(barrier, peers)
    for k in range(4):
        for link in range(2):
            ag(link, k).start()
    for step in direct:
        to, there = behind(step)
        pl.when(there)(functools.partial(
            pl.semaphore_signal, z_ready, inc=1, device_id=to, device_id_type=MESH
        ))

    r = lax.broadcasted_iota(jnp.int32, (rows, head), 0)
    lane = lax.broadcasted_iota(jnp.int32, (rows, head), 1)
    at_row = c * rows + (r // quarter) % 2 * half + r // half * quarter + r % quarter
    which = (lane % (head // 2)).astype(jnp.float32)
    angles = at_row.astype(jnp.float32) * jnp.exp(which * (-math.log(10000.0) / (head // 2)))
    cos[...] = jnp.cos(angles)
    sin[...] = jnp.where(lane < head // 2, -1.0, 1.0) * jnp.sin(angles)

    for d in small_loads:
        d.wait()
    for wide, i in ((pre, 0), (post, 1)):
        wide[...] = jnp.concatenate([small[i, k : k + 1, :] for k in range(small.shape[1])], axis=1)

    def norm(u, h):
        def body(i, carry):
            a, at = i // (quarter // 16), pl.ds(pl.multiple_of(i % (quarter // 16) * 16, 16), 16)
            v = nb[u, a, h, at, :].astype(jnp.float32)
            mean_sq = jnp.mean(v * v, axis=-1, keepdims=True)
            to = pl.ds(pl.multiple_of(h * half + i * 16, 16), 16)
            nrm[to, :] = (v * lax.rsqrt(mean_sq + epsilon) * pre[...]).astype(jnp.bfloat16)
            return carry

        lax.fori_loop(0, half // 16, body, 0)

    def z_copy(u, h, dz, step):
        return remote(
            kv.at[u, dz, p, :, h], kv.at[u, dz + step, p, :, h],
            z_s.at[u, h, dz + step], z_r.at[u, h, dz + step], ahead(step)[0],
        )

    def b_copy(u, h, dz):
        return remote(kv.at[u, dz, p, :, h], kv.at[u, dz, p, :, h], b_s.at[u, h, dz], b_r.at[u, h, dz], sib)

    def kv_arrived(u, h, dz):
        at = kv.at[u, dz, p, :, h]
        return remote(at, at, z_s.at[u, h, dz], z_r.at[u, h, dz], behind(1)[0])

    def kv_paired(u, h, dz):
        at = kv.at[u, dz, 1 - p, :, h]
        return remote(at, at, b_s.at[u, h, dz], b_r.at[u, h, dz], sib)

    def own_copies(u, h, act):
        for step in direct:
            @pl.when(ahead(step)[1])
            def _():
                act(z_copy(u, h, 0, step))

        @pl.when(p == 0)
        def _():
            act(b_copy(u, h, 0))

    def send_own(u, h):
        own_copies(u, h, lambda d: d.start())

    def passed_copies(u, h, dz, act):
        if dz in direct and dz + 1 <= reach:
            @pl.when(ahead(1)[1])
            def _():
                act(z_copy(u, h, dz, 1))

        act(b_copy(u, h, dz))

    def relay(u, h, dz):
        if dz > reach:
            return

        @pl.when(z >= dz)
        def _():
            kv_arrived(u, h, dz).wait_recv()
            passed_copies(u, h, dz, lambda d: d.start())

    farthest = jnp.minimum(z, reach)

    def share(units, dz):
        for u in units:
            for h in range(2):
                kv_arrived(u, h, dz).wait_recv()
                for step in direct:
                    if step > 1 and step + 1 <= reach:
                        pl.when((dz == step) & ahead(1)[1])(z_copy(u, h, step, 1).start)
                b_copy(u, h, dz).start()

    def wait_pairs(units, dz):
        for u in units:
            for h in range(2):
                kv_paired(u, h, dz).wait_recv()

    k_step = column_step(2 * kw, 256)
    q_step = column_step(qw, 256)

    def columns_of(lo, size, first, count, step):
        def columns(j, carry):
            at = pl.ds(pl.multiple_of(first + j * step, 128), step)
            raw[lo : lo + size, at] = jnp.dot(nrm[lo : lo + size, :], w[:, at], preferred_element_type=jnp.float32)
            return carry

        lax.fori_loop(0, count // step, columns, 0)

    def rotated(lo, size, col, gain):
        v = raw[lo : lo + size, col : col + head]
        mean_sq = jnp.mean(v * v, axis=-1, keepdims=True)
        v = v * lax.rsqrt(mean_sq + epsilon) * gain
        v = v * cos[lo : lo + size, :] + pltpu.roll(v, head // 2, 1) * sin[lo : lo + size, :]
        return v.astype(jnp.bfloat16)

    def project_keys(u, h):
        lo = h * half
        columns_of(lo, half, qw, 2 * kw, k_step)
        for g in range(kv_heads):
            keys = rotated(lo, half, qw + g * head, gains[1])
            for a in range(2):
                kv[u, 0, p, a, h, :, g * head : (g + 1) * head] = keys[a * quarter : (a + 1) * quarter]
        for a in range(2):
            at = slice(lo + a * quarter, lo + (a + 1) * quarter)
            kv[u, 0, p, a, h, :, kw:] = raw[at, qw + kw :].astype(jnp.bfloat16)

    def project_queries(u):
        columns_of(0, rows, 0, qw, q_step)
        for g in range(q_heads):
            found = rotated(0, rows, g * head, gains[0])
            for h in range(2):
                for a in range(2):
                    to, at = a * half + h * quarter, (2 * h + a) * quarter
                    q[u, to : to + quarter, g * head : (g + 1) * head] = found[at : at + quarter]

    def merged(parts):
        return jnp.concatenate(parts, axis=0)

    def attention(u, fresh):
        own, other = halves_of[u], halves_of[(0, 2, 1, 3)[u]]
        spans = [(0, rows, own)] if own == other else [(0, half, own), (half, half, other)]
        streams = [
            (i * kv_heads + g, g, lo, size, units)
            for i, (lo, size, units) in enumerate(spans) for g in range(kv_heads)
        ]

        def places(lo, size):
            qi = lax.broadcasted_iota(jnp.int32, (group, size, rows), 1).reshape(group * size, rows) + lo
            return qi, lax.broadcasted_iota(jnp.int32, (group * size, rows), 1)

        def block(units, dz, par, cols):
            return merged([
                kv[units[a], dz, par, a, h, :, cols] for a in range(2) for h in range(2)
            ])

        def step(dz, pars, mask, first=False):
            for n, g, lo, size, units in streams:
                kc = slice(g * head, (g + 1) * head)
                vc = slice(kw + g * head, kw + (g + 1) * head)
                at = slice(0, group * size)
                queries = merged([
                    q[u, lo : lo + size, h * head : (h + 1) * head] for h in range(g * group, (g + 1) * group)
                ])
                keys = merged([block(units, dz, par, kc) for par in pars])
                values = merged([block(units, dz, par, vc) for par in pars])
                s = lax.dot_general(queries, keys, (((1,), (1,)), ((), ())), preferred_element_type=jnp.float32)
                e = jnp.exp(s * score_scale)
                if mask is not None:
                    e = jnp.where(mask(lo, size), e, 0.0)
                total = sum(e[:, i * rows : (i + 1) * rows] for i in range(len(pars)))
                acc = jnp.dot(e.astype(jnp.bfloat16), values, preferred_element_type=jnp.float32)
                if first:
                    sums[n, at], accs[n, at] = total, acc
                else:
                    sums[n, at] += total
                    accs[n, at] += acc

        def causal(lo, size):
            qi, kj = places(lo, size)
            return kj <= qi

        def begin():
            step(0, [p], causal, True)

            def beside(_, carry):
                wait_pairs(fresh, 0)
                step(0, [0], None)
                return carry

            lax.fori_loop(0, p, beside, 0)

        def order(k):
            return jnp.where(k == 1, 1, farthest + 2 - k)

        def earlier(k, carry):
            dz = order(k)

            def near(lo, size):
                qi, kj = places(lo, size)
                apart = (p + 2 * dz) * rows + qi - kj
                return jnp.concatenate([apart, apart - rows], axis=1) < window

            pl.when(k < farthest)(lambda: share(fresh, order(k + 1)))
            wait_pairs(fresh, dz)
            step(dz, [0, 1], near if n_ctx * rows > window else None)
            return carry

        def complete():
            lax.fori_loop(1, farthest + 1, earlier, 0)
            for n, g, lo, size, _ in streams:
                at = slice(0, group * size)
                o = (accs[n, at] / jnp.sum(sums[n, at], axis=-1, keepdims=True)).astype(jnp.bfloat16)
                for i in range(group):
                    h = g * group + i
                    att[u, lo : lo + size, h * head : (h + 1) * head] = o[i * size : (i + 1) * size]

        return begin, complete

    def attend(u, fresh):
        for part in attention(u, fresh):
            part()

    blocks = features // o_step

    def output(u, first=0, last=blocks):
        def columns(j, carry):
            at = pl.ds(pl.multiple_of(j * o_step, o_step), o_step)
            pb[u, :, at] = jnp.dot(att[u], wo[:, at], preferred_element_type=jnp.float32).astype(jnp.bfloat16)
            return carry

        lax.fori_loop(first, last, columns, 0)

    spread = [pl.ds(i * o_step, (j - i) * o_step) for i, j in zip(cuts[:-1], cuts[1:])]

    def unit_copy(link, j):
        at = (pl.ds(link * half, half), spread[j])
        return remote(
            pb.at[(1, *at)], (rx, ry)[link].at[at], un_s.at[link, j], un_r.at[link, j], (x_to, y_to)[link]
        )

    def far_columns(link, j):
        at = (pl.ds(link * half, quarter), spread[j])
        return remote(pb.at[(3, *at)], dg.at[at], dc_s.at[link, j], dc_r.at[link, j], (x_to, y_to)[link])

    def far_rows(link, i):
        at = pl.ds(link * half + quarter + i * 16, 16)
        return remote(pb.at[3, at], dg.at[at], dr_s.at[link, i], dr_r.at[link, i], (x_to, y_to)[link])

    def sum_copy(link, i):
        at = pl.ds((1 - link) * half + i * 16, 16)
        return remote(pb.at[2, at], (rx, ry)[link].at[at], cb_s.at[link, i], cb_r.at[link, i], (x_to, y_to)[link])

    def both(copy, i, act="start"):
        for link in range(2):
            getattr(copy(link, i), act)()

    def every(copy, count, act):
        for i in range(count):
            both(copy, i, act)

    def output_and_send(u, copy, between=None):
        done = 0
        for i, stop in enumerate(cuts[1:]):
            upto = min(stop + 1, blocks)
            output(u, done, upto)
            both(copy, i)
            done = upto
            if i == 0 and between is not None:
                between()

    def add_rows(at):
        pb[2, at, :] = (pb[2, at, :].astype(jnp.float32) + dg[at, :].astype(jnp.float32)).astype(jnp.bfloat16)

    def arrive(u, h, between=None):
        both(ag, 2 * (u - 1) + h, "wait_recv")
        if u == 1:
            both(ag, 4 + h)
        norm(u, h)
        if between is not None:
            between()
        project_keys(u, h)
        send_own(u, h)

    tok_load.wait()
    norm(0, 0)
    norm(0, 1)
    for d in w_loads[:4]:
        d.wait()
    project_keys(0, 0)
    pl.when(readers > 0)(lambda: pl.semaphore_wait(z_ready, readers))
    send_own(0, 0)
    project_keys(0, 1)
    for d in w_loads[4:]:
        d.wait()
    project_queries(0)
    arrive(1, 0)
    relay(0, 0, 1)
    arrive(1, 1)
    relay(1, 0, 1)
    project_queries(1)
    relay(1, 1, 1)
    arrive(2, 0)
    wo_load.wait()
    arrive(2, 1, lambda: relay(2, 0, 1))
    project_queries(2)
    begin, complete = attention(1, (1, 2))
    begin()
    relay(2, 1, 1)
    arrive(3, 0)
    complete()
    output_and_send(1, unit_copy, lambda: arrive(3, 1, lambda: relay(3, 0, 1)))
    attend(2, ())
    relay(3, 1, 1)
    send_own(0, 1)
    project_queries(3)
    attend(3, (3,))
    output_and_send(3, far_columns)
    for i in range(quarter // 16):
        both(far_rows, i)
    relay(0, 1, 1)
    output(2)
    attend(0, (0,))

    every(far_columns, len(spread), "wait_recv")
    tiles = half // 16
    for i in range(tiles):
        if i >= tiles // 2:
            both(far_rows, i - tiles // 2, "wait_recv")
        for a in range(2):
            add_rows(pl.ds(a * half + i * 16, 16))
        both(sum_copy, i)
    output(0)

    every(unit_copy, len(spread), "wait_recv")
    for i in range(tiles):
        both(sum_copy, i, "wait_recv")
        for a in range(2):
            at = pl.ds(a * half + i * 16, 16)
            summed = pb[0, at, :].astype(jnp.float32) + rx[at, :].astype(jnp.float32) + ry[at, :].astype(jnp.float32)
            mean_sq = jnp.mean(summed * summed, axis=-1, keepdims=True)
            normed = summed * lax.rsqrt(mean_sq + epsilon) * post[...]
            mine = nb[0, a, i * 16 // quarter, pl.ds(i * 16 % quarter, 16), :].astype(jnp.float32)
            out_ref[at, :] = (mine + normed).astype(jnp.bfloat16)

    for k in range(6):
        both(ag, k, "wait_send")
    every(unit_copy, len(spread), "wait_send")
    every(far_columns, len(spread), "wait_send")
    for i in range(quarter // 16):
        both(far_rows, i, "wait_send")
    for i in range(tiles):
        both(sum_copy, i, "wait_send")
    for u in range(4):
        for h in range(2):
            own_copies(u, h, lambda d: d.wait_send())
            for dz in range(1, reach + 1):
                @pl.when(z >= dz)
                def _():
                    passed_copies(u, h, dz, lambda d: d.wait_send())


def per_device(
    n_ctx, tokens, pre_gain, w_query, key_weight, value_weight, query_norm_gain, key_gain, w_out, post_gain
):
    _, rows, features = tokens.shape
    head = query_norm_gain.shape[0]
    qw, kw = w_query.shape[1], key_weight.shape[1]
    reach = min(n_ctx // 2 - 1, -(-window // (2 * rows)))
    o_step = column_step(features, 768)
    blocks, tiles, quarter = features // o_step, rows // 32, rows // 4
    cuts = sorted({0, min(3, blocks), blocks})
    ranges = len(cuts) - 1
    any_spec = pl.BlockSpec(memory_space=pl.ANY)
    bf16, f32 = jnp.bfloat16, jnp.float32
    dma = pltpu.SemaphoreType.DMA
    out = pl.pallas_call(
        functools.partial(layer_kernel, n_ctx, reach, qw // head, kw // head, head, o_step, cuts),
        out_shape=pltpu.VMEM((rows, features), bf16),
        in_specs=[any_spec] * 9,
        out_specs=pl.BlockSpec(memory_space=pltpu.VMEM),
        scratch_shapes=[
            pltpu.VMEM((features, qw + 2 * kw), bf16),
            pltpu.VMEM((qw, features), bf16),
            pltpu.VMEM((4, 2, 2, quarter, features), bf16),
            pltpu.VMEM((rows, features), bf16),
            pltpu.VMEM((rows, qw + 2 * kw), f32),
            pltpu.VMEM((4, rows, qw), bf16),
            pltpu.VMEM((4, reach + 1, 2, 2, 2, quarter, 2 * kw), bf16),
            pltpu.VMEM((4, rows, qw), bf16),
            pltpu.VMEM((4, rows, features), bf16),
            pltpu.VMEM((rows, features), bf16),
            pltpu.VMEM((rows, features), bf16),
            pltpu.VMEM((rows, features), bf16),
            pltpu.VMEM((2, features // 128, 128), f32),
            pltpu.VMEM((2, 1, head), f32),
            pltpu.VMEM((1, features), f32),
            pltpu.VMEM((1, features), f32),
            pltpu.VMEM((rows, head), f32),
            pltpu.VMEM((rows, head), f32),
            pltpu.VMEM((2 * kw // head, qw // kw * rows, head), f32),
            pltpu.VMEM((2 * kw // head, qw // kw * rows, rows), f32),
            dma((12,)), dma((2, 6)), dma((2, 6)),
            dma((2, ranges)), dma((2, ranges)), dma((2, ranges)), dma((2, ranges)),
            dma((2, tiles // 2)), dma((2, tiles // 2)), dma((2, tiles)), dma((2, tiles)),
            dma((4, 2, reach + 1)), dma((4, 2, reach + 1)), dma((4, 2, reach + 1)), dma((4, 2, reach + 1)),
            pltpu.SemaphoreType.REGULAR,
        ],
        compiler_params=pltpu.CompilerParams(
            collective_id=0, has_side_effects=True, vmem_limit_bytes=vmem_limit
        ),
    )(
        tokens.reshape(2, 2, quarter, features), w_query, key_weight, value_weight, w_out,
        pre_gain.reshape(-1, 128), post_gain.reshape(-1, 128), query_norm_gain[None], key_gain[None],
    )
    return out[None]


def solution(mesh):
    return jax.shard_map(
        functools.partial(per_device, mesh.shape["ctx"]),
        mesh=mesh,
        in_specs=(
            P("fsdp", "ctx", None),
            P(),
            P(None, "fsdp"),
            P(None, "fsdp"),
            P(None, "fsdp"),
            P(),
            P(),
            P("fsdp", None),
            P(),
        ),
        out_specs=P("fsdp", "ctx", None),
        check_vma=False,
    )
```

```python
import functools
import math

import jax
import jax.numpy as jnp
from jax import lax
from jax.experimental import pallas as pl
from jax.experimental.pallas import tpu as pltpu
from jax.sharding import PartitionSpec as P

epsilon = 1e-06
score_scale = 168.0 ** (-0.5)
window = 1024
vmem_limit = 58_000_000
MESH = pl.DeviceIdType.MESH
halves_of = ((0, 0), (1, 2), (2, 1), (3, 3))


def column_step(total, limit):
    step = 128
    for count in range(1, limit // 128 + 1):
        if total % (count * 128) == 0:
            step = count * 128
    return step


def layer_kernel(
    n_ctx, reach, q_heads, kv_heads, head, o_step, cuts,
    tok_hbm, wq_hbm, wk_hbm, wv_hbm, wo_hbm, pre_hbm, post_hbm, qg_hbm, kg_hbm,
    out_ref,
    w, wo, nb, nrm, raw, q, kv, att, pb, rx, ry, dg, small, gains, pre, post, cos, sin, accs, sums,
    load_sem, ag_s, ag_r, un_s, un_r, dc_s, dc_r, dr_s, dr_r, cb_s, cb_r, z_s, z_r, b_s, b_r, z_ready,
):
    f = lax.axis_index("fsdp")
    c = lax.axis_index("ctx")
    quarter, features = nb.shape[3:]
    half, rows = 2 * quarter, 4 * quarter
    z = c // 2
    p = c % 2
    nz = n_ctx // 2
    x_to = {"fsdp": f + 1 - 2 * (f % 2)}
    y_to = {"fsdp": (f + 2) % 4}
    sib = {"ctx": c + 1 - 2 * p}

    def ahead(step):
        return {"ctx": lax.rem(c + 2 * step, n_ctx)}, z + step < nz

    def behind(step):
        return {"ctx": lax.rem(c + n_ctx - 2 * step, n_ctx)}, z >= step

    direct = [step for step in (1, 3) if step <= reach]
    qw, kw = q_heads * head, kv_heads * head
    group = q_heads // kv_heads

    barrier = pltpu.get_barrier_semaphore()
    for to in (x_to, y_to, sib):
        pl.semaphore_signal(barrier, inc=1, device_id=to, device_id_type=MESH)
    peers, readers = 3, 0
    for step in direct:
        to, there = ahead(step)
        pl.when(there)(functools.partial(
            pl.semaphore_signal, barrier, inc=1, device_id=to, device_id_type=MESH
        ))
        peers = peers + jnp.clip(z - step + 1, 0, 1)
        readers = readers + jnp.clip(nz - z - step, 0, 1)

    def load(i, src, dst):
        return pltpu.make_async_copy(src, dst, load_sem.at[i])

    tok_load = load(0, tok_hbm, nb.at[0])
    small_loads = [
        load(1, pre_hbm, small.at[0]), load(2, post_hbm, small.at[1]),
        load(3, qg_hbm, gains.at[0]), load(4, kg_hbm, gains.at[1]),
    ]
    cut = features // 2
    w_loads = []
    for j, (src, lo, wide) in enumerate(((wk_hbm, qw, kw), (wv_hbm, qw + kw, kw), (wq_hbm, 0, qw))):
        for part in range(2):
            rs = pl.ds(part * cut, cut)
            w_loads.append(load(5 + 2 * j + part, src.at[rs], w.at[rs, pl.ds(lo, wide)]))
    wo_load = load(11, wo_hbm, wo)
    for d in [tok_load] + small_loads + w_loads + [wo_load]:
        d.start()

    def remote(src, dst, s, r, to):
        return pltpu.make_async_remote_copy(
            src_ref=src, dst_ref=dst, send_sem=s, recv_sem=r, device_id=to, device_id_type=MESH
        )

    def ag(link, k):
        part, h = k // 2, k % 2
        a = (link, 1 - link, 1 - link)[part]
        src = tok_hbm.at[a, h] if part < 2 else nb.at[1, a, h]
        return remote(src, nb.at[part + 1, a, h], ag_s.at[link, k], ag_r.at[link, k], (x_to, y_to)[link])

    pl.semaphore_wait(barrier, peers)
    for k in range(4):
        for link in range(2):
            ag(link, k).start()
    for step in direct:
        to, there = behind(step)
        pl.when(there)(functools.partial(
            pl.semaphore_signal, z_ready, inc=1, device_id=to, device_id_type=MESH
        ))

    r = lax.broadcasted_iota(jnp.int32, (rows, head), 0)
    lane = lax.broadcasted_iota(jnp.int32, (rows, head), 1)
    at_row = c * rows + (r // quarter) % 2 * half + r // half * quarter + r % quarter
    which = (lane % (head // 2)).astype(jnp.float32)
    angles = at_row.astype(jnp.float32) * jnp.exp(which * (-math.log(10000.0) / (head // 2)))
    cos[...] = jnp.cos(angles)
    sin[...] = jnp.where(lane < head // 2, -1.0, 1.0) * jnp.sin(angles)

    for d in small_loads:
        d.wait()
    for wide, i in ((pre, 0), (post, 1)):
        wide[...] = jnp.concatenate([small[i, k : k + 1, :] for k in range(small.shape[1])], axis=1)

    def norm(u, h):
        def body(i, carry):
            a, at = i // (quarter // 16), pl.ds(pl.multiple_of(i % (quarter // 16) * 16, 16), 16)
            v = nb[u, a, h, at, :].astype(jnp.float32)
            mean_sq = jnp.mean(v * v, axis=-1, keepdims=True)
            to = pl.ds(pl.multiple_of(h * half + i * 16, 16), 16)
            nrm[to, :] = (v * lax.rsqrt(mean_sq + epsilon) * pre[...]).astype(jnp.bfloat16)
            return carry

        lax.fori_loop(0, half // 16, body, 0)

    def z_copy(u, h, dz, step):
        return remote(
            kv.at[u, dz, p, :, h], kv.at[u, dz + step, p, :, h],
            z_s.at[u, h, dz + step], z_r.at[u, h, dz + step], ahead(step)[0],
        )

    def b_copy(u, h, dz):
        return remote(kv.at[u, dz, p, :, h], kv.at[u, dz, p, :, h], b_s.at[u, h, dz], b_r.at[u, h, dz], sib)

    def kv_arrived(u, h, dz):
        at = kv.at[u, dz, p, :, h]
        return remote(at, at, z_s.at[u, h, dz], z_r.at[u, h, dz], behind(1)[0])

    def kv_paired(u, h, dz):
        at = kv.at[u, dz, 1 - p, :, h]
        return remote(at, at, b_s.at[u, h, dz], b_r.at[u, h, dz], sib)

    def own_copies(u, h, act):
        for step in direct:
            @pl.when(ahead(step)[1])
            def _():
                act(z_copy(u, h, 0, step))

        @pl.when(p == 0)
        def _():
            act(b_copy(u, h, 0))

    def send_own(u, h):
        own_copies(u, h, lambda d: d.start())

    def passed_copies(u, h, dz, act):
        if dz in direct and dz + 1 <= reach:
            @pl.when(ahead(1)[1])
            def _():
                act(z_copy(u, h, dz, 1))

        act(b_copy(u, h, dz))

    def relay(u, h, dz):
        if dz > reach:
            return

        @pl.when(z >= dz)
        def _():
            kv_arrived(u, h, dz).wait_recv()
            passed_copies(u, h, dz, lambda d: d.start())

    farthest = jnp.minimum(z, reach)

    def share(units, dz):
        for u in units:
            for h in range(2):
                kv_arrived(u, h, dz).wait_recv()
                for step in direct:
                    if step > 1 and step + 1 <= reach:
                        pl.when((dz == step) & ahead(1)[1])(z_copy(u, h, step, 1).start)
                b_copy(u, h, dz).start()

    def wait_pairs(units, dz):
        for u in units:
            for h in range(2):
                kv_paired(u, h, dz).wait_recv()

    k_step = column_step(2 * kw, 256)
    q_step = column_step(qw, 256)

    def columns_of(lo, size, first, count, step):
        def columns(j, carry):
            at = pl.ds(pl.multiple_of(first + j * step, 128), step)
            raw[lo : lo + size, at] = jnp.dot(nrm[lo : lo + size, :], w[:, at], preferred_element_type=jnp.float32)
            return carry

        lax.fori_loop(0, count // step, columns, 0)

    def rotated(lo, size, col, gain):
        v = raw[lo : lo + size, col : col + head]
        mean_sq = jnp.mean(v * v, axis=-1, keepdims=True)
        v = v * lax.rsqrt(mean_sq + epsilon) * gain
        v = v * cos[lo : lo + size, :] + pltpu.roll(v, head // 2, 1) * sin[lo : lo + size, :]
        return v.astype(jnp.bfloat16)

    def project_keys(u, h):
        lo = h * half
        columns_of(lo, half, qw, 2 * kw, k_step)
        for g in range(kv_heads):
            keys = rotated(lo, half, qw + g * head, gains[1])
            for a in range(2):
                kv[u, 0, p, a, h, :, g * head : (g + 1) * head] = keys[a * quarter : (a + 1) * quarter]
        for a in range(2):
            at = slice(lo + a * quarter, lo + (a + 1) * quarter)
            kv[u, 0, p, a, h, :, kw:] = raw[at, qw + kw :].astype(jnp.bfloat16)

    def project_queries(u):
        columns_of(0, rows, 0, qw, q_step)
        for g in range(q_heads):
            found = rotated(0, rows, g * head, gains[0])
            for h in range(2):
                for a in range(2):
                    to, at = a * half + h * quarter, (2 * h + a) * quarter
                    q[u, to : to + quarter, g * head : (g + 1) * head] = found[at : at + quarter]

    def merged(parts):
        return jnp.concatenate(parts, axis=0)

    def attention(u, fresh):
        own, other = halves_of[u], halves_of[(0, 2, 1, 3)[u]]
        spans = [(0, rows, own)] if own == other else [(0, half, own), (half, half, other)]
        streams = [
            (i * kv_heads + g, g, lo, size, units)
            for i, (lo, size, units) in enumerate(spans) for g in range(kv_heads)
        ]

        def places(lo, size):
            qi = lax.broadcasted_iota(jnp.int32, (group, size, rows), 1).reshape(group * size, rows) + lo
            return qi, lax.broadcasted_iota(jnp.int32, (group * size, rows), 1)

        def block(units, dz, par, cols):
            return merged([
                kv[units[a], dz, par, a, h, :, cols] for a in range(2) for h in range(2)
            ])

        def step(dz, pars, mask, first=False):
            for n, g, lo, size, units in streams:
                kc = slice(g * head, (g + 1) * head)
                vc = slice(kw + g * head, kw + (g + 1) * head)
                at = slice(0, group * size)
                queries = merged([
                    q[u, lo : lo + size, h * head : (h + 1) * head] for h in range(g * group, (g + 1) * group)
                ])
                keys = merged([block(units, dz, par, kc) for par in pars])
                values = merged([block(units, dz, par, vc) for par in pars])
                s = lax.dot_general(queries, keys, (((1,), (1,)), ((), ())), preferred_element_type=jnp.float32)
                e = jnp.exp(s * score_scale)
                if mask is not None:
                    e = jnp.where(mask(lo, size), e, 0.0)
                total = sum(e[:, i * rows : (i + 1) * rows] for i in range(len(pars)))
                acc = jnp.dot(e.astype(jnp.bfloat16), values, preferred_element_type=jnp.float32)
                if first:
                    sums[n, at], accs[n, at] = total, acc
                else:
                    sums[n, at] += total
                    accs[n, at] += acc

        def causal(lo, size):
            qi, kj = places(lo, size)
            return kj <= qi

        def begin():
            step(0, [p], causal, True)

            def beside(_, carry):
                wait_pairs(fresh, 0)
                step(0, [0], None)
                return carry

            lax.fori_loop(0, p, beside, 0)

        def order(k):
            return jnp.where(k == 1, 1, farthest + 2 - k)

        def earlier(k, carry):
            dz = order(k)

            def near(lo, size):
                qi, kj = places(lo, size)
                apart = (p + 2 * dz) * rows + qi - kj
                return jnp.concatenate([apart, apart - rows], axis=1) < window

            pl.when(k < farthest)(lambda: share(fresh, order(k + 1)))
            wait_pairs(fresh, dz)
            step(dz, [0, 1], near if n_ctx * rows > window else None)
            return carry

        def complete():
            lax.fori_loop(1, farthest + 1, earlier, 0)
            for n, g, lo, size, _ in streams:
                at = slice(0, group * size)
                o = (accs[n, at] / jnp.sum(sums[n, at], axis=-1, keepdims=True)).astype(jnp.bfloat16)
                for i in range(group):
                    h = g * group + i
                    att[u, lo : lo + size, h * head : (h + 1) * head] = o[i * size : (i + 1) * size]

        return begin, complete

    def attend(u, fresh):
        for part in attention(u, fresh):
            part()

    blocks = features // o_step

    def output(u, first=0, last=blocks):
        def columns(j, carry):
            at = pl.ds(pl.multiple_of(j * o_step, o_step), o_step)
            pb[u, :, at] = jnp.dot(att[u], wo[:, at], preferred_element_type=jnp.float32).astype(jnp.bfloat16)
            return carry

        lax.fori_loop(first, last, columns, 0)

    spread = [pl.ds(i * o_step, (j - i) * o_step) for i, j in zip(cuts[:-1], cuts[1:])]

    def unit_copy(link, j):
        at = (pl.ds(link * half, half), spread[j])
        return remote(
            pb.at[(1, *at)], (rx, ry)[link].at[at], un_s.at[link, j], un_r.at[link, j], (x_to, y_to)[link]
        )

    def far_columns(link, j):
        at = (pl.ds(link * half, quarter), spread[j])
        return remote(pb.at[(3, *at)], dg.at[at], dc_s.at[link, j], dc_r.at[link, j], (x_to, y_to)[link])

    def far_rows(link, i):
        at = pl.ds(link * half + quarter + i * 16, 16)
        return remote(pb.at[3, at], dg.at[at], dr_s.at[link, i], dr_r.at[link, i], (x_to, y_to)[link])

    def sum_copy(link, i):
        at = pl.ds((1 - link) * half + i * 16, 16)
        return remote(pb.at[2, at], (rx, ry)[link].at[at], cb_s.at[link, i], cb_r.at[link, i], (x_to, y_to)[link])

    def both(copy, i, act="start"):
        for link in range(2):
            getattr(copy(link, i), act)()

    def every(copy, count, act):
        for i in range(count):
            both(copy, i, act)

    def output_and_send(u, copy, between=None):
        done = 0
        for i, stop in enumerate(cuts[1:]):
            upto = min(stop + 1, blocks)
            output(u, done, upto)
            both(copy, i)
            done = upto
            if i == 0 and between is not None:
                between()

    def add_rows(at):
        pb[2, at, :] = (pb[2, at, :].astype(jnp.float32) + dg[at, :].astype(jnp.float32)).astype(jnp.bfloat16)

    def arrive(u, h, between=None):
        both(ag, 2 * (u - 1) + h, "wait_recv")
        if u == 1:
            both(ag, 4 + h)
        norm(u, h)
        if between is not None:
            between()
        project_keys(u, h)
        send_own(u, h)

    tok_load.wait()
    norm(0, 0)
    norm(0, 1)
    for d in w_loads[:4]:
        d.wait()
    project_keys(0, 0)
    pl.when(readers > 0)(lambda: pl.semaphore_wait(z_ready, readers))
    send_own(0, 0)
    project_keys(0, 1)
    for d in w_loads[4:]:
        d.wait()
    project_queries(0)
    arrive(1, 0)
    relay(0, 0, 1)
    arrive(1, 1)
    relay(1, 0, 1)
    project_queries(1)
    relay(1, 1, 1)
    arrive(2, 0)
    wo_load.wait()
    arrive(2, 1, lambda: relay(2, 0, 1))
    project_queries(2)
    begin, complete = attention(1, (1, 2))
    begin()
    relay(2, 1, 1)
    arrive(3, 0)
    complete()
    output_and_send(1, unit_copy, lambda: arrive(3, 1, lambda: relay(3, 0, 1)))
    attend(2, ())
    relay(3, 1, 1)
    send_own(0, 1)
    project_queries(3)
    attend(3, (3,))
    output_and_send(3, far_columns)
    for i in range(quarter // 16):
        both(far_rows, i)
    relay(0, 1, 1)
    output(2)

    every(far_columns, len(spread), "wait_recv")
    tiles = half // 16
    for i in range(tiles):
        if i >= tiles // 2:
            both(far_rows, i - tiles // 2, "wait_recv")
        for a in range(2):
            add_rows(pl.ds(a * half + i * 16, 16))
        both(sum_copy, i)
    attend(0, (0,))
    output(0)

    every(unit_copy, len(spread), "wait_recv")
    for i in range(tiles):
        both(sum_copy, i, "wait_recv")
        for a in range(2):
            at = pl.ds(a * half + i * 16, 16)
            summed = pb[0, at, :].astype(jnp.float32) + rx[at, :].astype(jnp.float32) + ry[at, :].astype(jnp.float32)
            mean_sq = jnp.mean(summed * summed, axis=-1, keepdims=True)
            normed = summed * lax.rsqrt(mean_sq + epsilon) * post[...]
            mine = nb[0, a, i * 16 // quarter, pl.ds(i * 16 % quarter, 16), :].astype(jnp.float32)
            out_ref[at, :] = (mine + normed).astype(jnp.bfloat16)

    for k in range(6):
        both(ag, k, "wait_send")
    every(unit_copy, len(spread), "wait_send")
    every(far_columns, len(spread), "wait_send")
    for i in range(quarter // 16):
        both(far_rows, i, "wait_send")
    for i in range(tiles):
        both(sum_copy, i, "wait_send")
    for u in range(4):
        for h in range(2):
            own_copies(u, h, lambda d: d.wait_send())
            for dz in range(1, reach + 1):
                @pl.when(z >= dz)
                def _():
                    passed_copies(u, h, dz, lambda d: d.wait_send())


def per_device(
    n_ctx, tokens, pre_gain, w_query, key_weight, value_weight, query_norm_gain, key_gain, w_out, post_gain
):
    _, rows, features = tokens.shape
    head = query_norm_gain.shape[0]
    qw, kw = w_query.shape[1], key_weight.shape[1]
    reach = min(n_ctx // 2 - 1, -(-window // (2 * rows)))
    o_step = column_step(features, 768)
    blocks, tiles, quarter = features // o_step, rows // 32, rows // 4
    cuts = sorted({0, min(3, blocks), blocks})
    ranges = len(cuts) - 1
    any_spec = pl.BlockSpec(memory_space=pl.ANY)
    bf16, f32 = jnp.bfloat16, jnp.float32
    dma = pltpu.SemaphoreType.DMA
    out = pl.pallas_call(
        functools.partial(layer_kernel, n_ctx, reach, qw // head, kw // head, head, o_step, cuts),
        out_shape=pltpu.VMEM((rows, features), bf16),
        in_specs=[any_spec] * 9,
        out_specs=pl.BlockSpec(memory_space=pltpu.VMEM),
        scratch_shapes=[
            pltpu.VMEM((features, qw + 2 * kw), bf16),
            pltpu.VMEM((qw, features), bf16),
            pltpu.VMEM((4, 2, 2, quarter, features), bf16),
            pltpu.VMEM((rows, features), bf16),
            pltpu.VMEM((rows, qw + 2 * kw), f32),
            pltpu.VMEM((4, rows, qw), bf16),
            pltpu.VMEM((4, reach + 1, 2, 2, 2, quarter, 2 * kw), bf16),
            pltpu.VMEM((4, rows, qw), bf16),
            pltpu.VMEM((4, rows, features), bf16),
            pltpu.VMEM((rows, features), bf16),
            pltpu.VMEM((rows, features), bf16),
            pltpu.VMEM((rows, features), bf16),
            pltpu.VMEM((2, features // 128, 128), f32),
            pltpu.VMEM((2, 1, head), f32),
            pltpu.VMEM((1, features), f32),
            pltpu.VMEM((1, features), f32),
            pltpu.VMEM((rows, head), f32),
            pltpu.VMEM((rows, head), f32),
            pltpu.VMEM((2 * kw // head, qw // kw * rows, head), f32),
            pltpu.VMEM((2 * kw // head, qw // kw * rows, rows), f32),
            dma((12,)), dma((2, 6)), dma((2, 6)),
            dma((2, ranges)), dma((2, ranges)), dma((2, ranges)), dma((2, ranges)),
            dma((2, tiles // 2)), dma((2, tiles // 2)), dma((2, tiles)), dma((2, tiles)),
            dma((4, 2, reach + 1)), dma((4, 2, reach + 1)), dma((4, 2, reach + 1)), dma((4, 2, reach + 1)),
            pltpu.SemaphoreType.REGULAR,
        ],
        compiler_params=pltpu.CompilerParams(
            collective_id=0, has_side_effects=True, vmem_limit_bytes=vmem_limit
        ),
    )(
        tokens.reshape(2, 2, quarter, features), w_query, key_weight, value_weight, w_out,
        pre_gain.reshape(-1, 128), post_gain.reshape(-1, 128), query_norm_gain[None], key_gain[None],
    )
    return out[None]


def solution(mesh):
    return jax.shard_map(
        functools.partial(per_device, mesh.shape["ctx"]),
        mesh=mesh,
        in_specs=(
            P("fsdp", "ctx", None),
            P(),
            P(None, "fsdp"),
            P(None, "fsdp"),
            P(None, "fsdp"),
            P(),
            P(),
            P("fsdp", None),
            P(),
        ),
        out_specs=P("fsdp", "ctx", None),
        check_vma=False,
    )
```
